32 devices in a mesh: lon: 8 (over y, x, core), lat: 4 (over z).
Axes of the slice: x: 2, y: 2, z: 4, core: 2. Of those that a mesh axis runs over, the one named last changes fastest.
Arguments:
- fields: float32 [5, 1, 128, 11520], P(None, None, 'lat', 'lon'), may hold values from -6 to 6
- frac_x: float32 [2, 1, 128], replicated, may hold values from 0.05 to 0.95
- frac_y: float32 [2, 1, 128], replicated, may hold values from 0.05 to 0.9
- shift_cells: int32 [2, 1, 128], replicated, may hold values from -5760 to 5759, as said below
- polar_mask: int32 [128], replicated, may hold values from 0 to 1, as said below
Outputs:
- fields_out: float32 [5, 1, 128, 11520], P(None, None, 'lat', 'lon')
The draws below stay inside these ranges and needn't reach their ends.
Inputs may be any that keep to these rules, and one draw needn't show every extreme that they name: `shift_cells`: outside the first and last 32 rows every count lies in -2 .. 1, and both -2 and 1 occur there. `polar_mask`: nonzero only in the first and last 32 rows; the first and the last row are 1.
All inputs are finite; a program needn't handle non-finite values.
Results may differ from the reference program's by a relative error of at most 0.00016.
Values sent between devices are 32-bit elements; how exact they have to be, the bound alone decides.
A program may use at most 64 MiB of HBM per device.

```python
import math
import jax
import jax.numpy as jnp

NFIELD = 5
SUBS = 2
REACH = 4
LEV = 1
CLAT = 32
NLON = 11520
CLON = 1440
NLAT = 128


def draw_shift_cells(key, part):
    key_big = jax.random.fold_in(key, 11)
    key_small = jax.random.fold_in(key, 12)
    shape = (SUBS, LEV, NLAT)
    big = jax.random.randint(key_big, shape, -REACH * CLON, REACH * CLON)
    small = jax.random.randint(key_small, shape, -2, 2)
    rows = jnp.arange(NLAT)
    polar = (rows < CLAT) | (rows >= NLAT - CLAT)
    counts = jnp.where(polar[None, None, :], big, small).astype(jnp.int32)
    counts = counts.at[0, 0, 0].set(REACH * CLON - 1)
    counts = counts.at[1, 0, NLAT - 1].set(-REACH * CLON)
    counts = counts.at[0, 0, CLAT].set(-2)
    counts = counts.at[1, 0, CLAT].set(1)
    return counts


def draw_polar_mask(key, part):
    picks = jax.random.randint(jax.random.fold_in(key, 21), (NLAT,), 0, 4)
    rows = jnp.arange(NLAT)
    polar = (rows < CLAT) | (rows >= NLAT - CLAT)
    marks = jnp.where(polar & (picks > 0), 1, 0)
    marks = marks.at[0].set(1).at[NLAT - 1].set(1)
    return marks.astype(jnp.int32)


def block_levels(own_key, shape, shards, low, high):
    def one(axis_at, parts):
        steps = jax.random.uniform(jax.random.fold_in(jax.random.fold_in(own_key, 6), axis_at), (parts,), jnp.float32, low / len(shards), high / len(shards))
        return jnp.repeat(jnp.exp(steps), shape[axis_at] // parts).reshape((-1,) + (1,) * (len(shape) - axis_at - 1))

    factor_of = one(*shards[0])
    for cut in shards[1:]:
        factor_of = factor_of * one(*cut)
    return factor_of


def gaussian(stream_key, shape, spread, most, pieces=(), kind=jnp.bfloat16):
    array = spread * jax.random.normal(stream_key, shape, jnp.float32)
    if pieces:
        array = array * block_levels(stream_key, shape, pieces, -0.22, 0.18)
    return jnp.clip(array, -most, most).astype(kind)


def setup_inputs(seed: int = 0) -> dict:
    seeds = jax.random.split(jax.random.key(seed), 6)
    return {
        "fields": gaussian(seeds[0], (NFIELD, LEV, NLAT, NLON), 1.0, 6.0, ((2, 4), (3, 8)), jnp.float32),
        "frac_x": jnp.clip(jax.random.uniform(seeds[1], (SUBS, LEV, NLAT), jnp.float32, 0.05, 0.95), 0.05, 0.95),
        "frac_y": jnp.clip(jax.random.uniform(seeds[2], (SUBS, LEV, NLAT), jnp.float32, 0.05, 0.9), 0.05, 0.9),
        "shift_cells": draw_shift_cells(jax.random.fold_in(seeds[5], 71), 0),
        "polar_mask": draw_polar_mask(jax.random.fold_in(seeds[5], 71), 0),
    }


def filter_gain(lat_rows):
    phi = math.pi * (lat_rows.astype(jnp.float32) + 0.5) / NLAT - math.pi / 2
    edge_cos = math.sin(math.pi * (CLAT - 0.5) / NLAT)
    b_val = jnp.cos(phi) / edge_cos
    waves = jnp.arange(NLON // 2 + 1, dtype=jnp.int32).astype(jnp.float32)
    sine = jnp.sin(math.pi * waves / NLON)
    return 1.0 / (1.0 + (sine[None, :] ** 2) / (b_val[:, None] ** 2))


def reference(fields, frac_x, frac_y, shift_cells, polar_mask):
    state = fields
    lon_ids = jnp.arange(NLON, dtype=jnp.int32)
    chosen = jnp.concatenate([jnp.arange(CLAT, dtype=jnp.int32), jnp.arange(NLAT - CLAT, NLAT, dtype=jnp.int32)])
    gain = filter_gain(chosen)
    keep = (polar_mask[chosen] == 1)[None, None, :, None]
    face_ids = jnp.arange(NLAT, dtype=jnp.int32)
    for substep in range(SUBS):
        courant = frac_x[substep][None, :, :, None]
        previous = jnp.roll(state, 1, axis=3)
        edge = state + 0.5 * (1.0 - courant) * (state - previous)
        zonal = state - courant * (edge - jnp.roll(edge, 1, axis=3))
        source = (lon_ids[None, None, :] - shift_cells[substep][:, :, None]) % NLON
        shifted = jax.vmap(lambda block: jnp.take_along_axis(block, source, axis=2))(zonal)
        polar_rows = shifted[:, :, chosen, :]
        spectrum = jnp.fft.rfft(polar_rows, axis=3)
        smoothed = jnp.fft.irfft(spectrum * gain[None, None, :, :], n=NLON, axis=3).astype(jnp.float32)
        polar_rows = jnp.where(keep, smoothed, polar_rows)
        filtered = shifted.at[:, :, chosen, :].set(polar_rows)
        merid = jnp.where(face_ids == 0, jnp.zeros_like(frac_y[substep]), frac_y[substep])[None, :, :, None]
        padded = jnp.pad(filtered, ((0, 0), (0, 0), (2, 0), (0, 0)))
        upper = padded[:, :, 1:NLAT + 1, :]
        lower = padded[:, :, 0:NLAT, :]
        flux = merid * (upper + 0.5 * (1.0 - merid) * (upper - lower))
        flux = jnp.concatenate([flux, jnp.zeros_like(flux[:, :, :1, :])], axis=2)
        state = filtered + flux[:, :, :NLAT, :] - flux[:, :, 1:, :]
    return state
```

```python
import functools
import math

import jax
import jax.numpy as jnp
import numpy as np
from jax import lax
from jax.experimental import pallas as pl
from jax.experimental.pallas import tpu as pltpu
from jax.sharding import PartitionSpec as P

SUBS = 2
LANES = 128
HALO = 2
MESH = pl.DeviceIdType.MESH
VMEM_LIMIT = 48 * 1024 * 1024


class Plan:
    def __init__(self, mesh, fields_shape):
        self.blocks = mesh.shape["lon"]
        self.bands = mesh.shape["lat"]
        self.fields, _, self.lat_total, self.lon_total = fields_shape
        self.lat = self.lat_total // self.bands
        self.lon = self.lon_total // self.blocks
        self.cols = -(-self.lon // LANES)
        self.rem = self.lon - LANES * (self.cols - 1)
        self.rows = self.fields * self.lat
        self.own = self.rows // self.blocks
        pitch = self.cols
        while (self.own * pitch) % 8 or (HALO * pitch) % 8:
            pitch += 1
        self.pitch = pitch
        self.slots = self.own + 2 * HALO
        self.unit = 2 if self.own % 2 == 0 else 1
        assert self.rows % self.blocks == 0 and self.own <= self.lat
        assert self.blocks & (self.blocks - 1) == 0 and self.blocks % 8 == 0 and self.lat % 8 == 0
        self.south_to = [
            (f, d)
            for f in range(self.fields)
            for d in sorted({f * self.lat // self.own, (f * self.lat + 1) // self.own})
        ]


def decay_table(plan):
    rows = np.arange(plan.lat_total, dtype=np.float64)
    phi = math.pi * (rows + 0.5) / plan.lat_total - math.pi / 2
    b = np.cos(phi) / math.sin(math.pi * (plan.lat - 0.5) / plan.lat_total)
    log_r = -2.0 * np.arcsinh(b)
    r = np.exp(log_r)
    lines = [np.exp(log_r * 2**k) for k in range(7)]
    lines += [np.exp(log_r * LANES), np.exp(log_r * plan.rem)]
    lines += [(1 - r) / (1 + r), 1 / (1 - np.exp(log_r * plan.lon_total)), log_r]
    lines += [np.exp(log_r * plan.lon * 2**k) for k in range(plan.blocks.bit_length() - 1)]
    table = np.stack(lines).astype(np.float32)
    return np.where(np.abs(table) < 1.2e-38, np.float32(0), table)


def spread_kernel(plan, x_ref, out_ref, packed, send, recv, south_send, south_recv, own_sem):
    me = lax.axis_index("lon")
    band = lax.axis_index("lat")
    blocks, pitch, own = plan.blocks, plan.pitch, plan.own
    packed[0 : HALO * pitch, :] = jnp.zeros((HALO * pitch, LANES), jnp.float32)

    def fill(group, carry):
        for c in range(plan.cols):
            width = LANES if c < plan.cols - 1 else plan.rem
            v = x_ref[pl.ds(pl.multiple_of(group * 8, 8), 8), c * LANES : c * LANES + width]
            if width < LANES:
                v = jnp.concatenate([v, jnp.zeros((8, LANES - width), jnp.float32)], axis=1)
            packed[pl.ds((group * 8 + HALO) * pitch + c, 8, stride=pitch), :] = v
        return carry

    lax.fori_loop(0, plan.rows // 8, fill, 0)
    main = (own + HALO) * pitch
    mine = pl.multiple_of(me * own * pitch, 8)
    local = pltpu.make_async_copy(
        packed.at[pl.ds(mine, main)], out_ref.at[me, pl.ds(0, main)], own_sem
    )
    local.start()
    copies = []
    for k in range(1, blocks):
        to = lax.rem(me + k, blocks)
        copy = pltpu.make_async_remote_copy(
            src_ref=packed.at[pl.ds(pl.multiple_of(to * own * pitch, 8), main)],
            dst_ref=out_ref.at[me, pl.ds(0, main)],
            send_sem=send.at[k],
            recv_sem=recv.at[k],
            device_id={"lon": to, "lat": band},
            device_id_type=MESH,
        )
        copy.start()
        copies.append(copy)

    def south(i):
        f, d = plan.south_to[i]
        first = (HALO + f * plan.lat + plan.lat - HALO) * pitch
        return pltpu.make_async_remote_copy(
            src_ref=packed.at[pl.ds(first, HALO * pitch)],
            dst_ref=out_ref.at[me, pl.ds(main, HALO * pitch)],
            send_sem=south_send.at[i],
            recv_sem=south_recv.at[me],
            device_id={"lon": jnp.int32(d), "lat": lax.rem(band + 1, plan.bands)},
            device_id_type=MESH,
        )

    @pl.when(band < plan.bands - 1)
    def _():
        for i in range(len(plan.south_to)):
            south(i).start()

    local.wait()
    for copy in copies:
        copy.wait()

    @pl.when(band < plan.bands - 1)
    def _():
        for i in range(len(plan.south_to)):
            south(i).wait_send()

    for d in sorted({d for _, d in plan.south_to}):

        @pl.when(jnp.logical_and(band > 0, me == d))
        def _():
            for source in range(blocks):
                pltpu.make_async_remote_copy(
                    src_ref=packed.at[pl.ds(0, HALO * pitch)],
                    dst_ref=out_ref.at[source, pl.ds(main, HALO * pitch)],
                    send_sem=south_send.at[0],
                    recv_sem=south_recv.at[source],
                    device_id={"lon": me, "lat": band - 1},
                    device_id_type=MESH,
                ).wait_recv()


def row_steps(plan, x, courant, count, marked, power, joined):
    blocks, cols, rem = plan.blocks, plan.cols, plan.rem
    lane = lax.broadcasted_iota(jnp.int32, (blocks, LANES), 1)
    tail = lane < rem
    x = x[:-1] + [jnp.where(tail, x[-1], 0.0)]

    half = 0.5 * (1.0 - courant)
    w0 = 1.0 - courant * (1.0 + half)
    w1 = courant * (1.0 + 2.0 * half)
    w2 = -courant * half
    west = pltpu.roll(x[-1], 1, 0)
    before1 = pltpu.roll(west, LANES + 1 - rem, 1) if rem > 1 else west
    before2 = pltpu.roll(west, LANES + 2 - rem, 1)
    zonal = []
    for c in range(cols):
        one, two = pltpu.roll(x[c], 1, 1), pltpu.roll(x[c], 2, 1)
        zonal.append(
            w0 * x[c]
            + w1 * jnp.where(lane < 1, before1, one)
            + w2 * jnp.where(lane < 2, before2, two)
        )
        before1, before2 = one, two

    count = jnp.where(count < 0, count + plan.lon_total, count)
    jump = count // plan.lon
    start = plan.lon - (count - jump * plan.lon)
    moved = [pltpu.roll(z, jump, 0) for z in zonal]
    western = [pltpu.roll(m, 1, 0) for m in moved]
    turned = [pltpu.roll(m, rem % LANES, 1) for m in moved]
    for c in range(cols - 1):
        joined[:, c * LANES : (c + 1) * LANES] = western[c]
    for c in range(cols + 1):
        left = western[-1] if c == 0 else turned[c - 1]
        right = turned[c] if c < cols else left
        at = (cols - 1 + c) * LANES
        joined[:, at : at + LANES] = jnp.where(tail, left, right)
    first = start // LANES
    within = start - first * LANES
    window = [
        joined[:, pl.ds(pl.multiple_of((first + c) * LANES, LANES), LANES)] for c in range(cols + 1)
    ]
    window = [pltpu.roll(w, lax.rem(LANES - within, LANES), 1) for w in window]
    keep = lane < LANES - within
    s = [jnp.where(keep, window[c], window[c + 1]) for c in range(cols)]
    s[-1] = jnp.where(tail, s[-1], 0.0)

    r128, r_rem, gain, closing, log_r = (power(7 + i) for i in range(5))
    ahead = [jnp.where(lane >= 1 << k, power(k), 0.0) for k in range(7)]
    back = [jnp.where(lane < LANES - (1 << k), power(k), 0.0) for k in range(7)]
    lane_f = lane.astype(jnp.float32)
    enter_west = jnp.exp(log_r * (lane_f + 1.0))
    enter_east = jnp.exp(log_r * (LANES - lane_f))
    enter_tail = jnp.exp(log_r * jnp.maximum(rem - lane_f, 0.0))
    p, q = [], []
    for c in range(cols):
        u, v = s[c], s[c]
        for k in range(7):
            u = u + ahead[k] * pltpu.roll(u, 1 << k, 1)
            v = v + back[k] * pltpu.roll(v, LANES - (1 << k), 1)
        p.append(u)
        q.append(v)

    def spread(column, at):
        return jnp.broadcast_to(column[:, at : at + 1], (blocks, LANES))

    ends = [spread(p[c], LANES - 1 if c < cols - 1 else rem - 1) for c in range(cols)]
    begins = [spread(q[c], 0) for c in range(cols)]

    def closed(total, sign):
        total = pltpu.roll(total, 1 if sign > 0 else blocks - 1, 0)
        for k in range(blocks.bit_length() - 1):
            by = 1 << k
            total = total + power(12 + k) * pltpu.roll(total, by if sign > 0 else blocks - by, 0)
        return total * closing

    total = ends[0]
    for c in range(1, cols):
        total = ends[c] + (r128 if c < cols - 1 else r_rem) * total
    carry = closed(total, 1)
    for c in range(cols):
        p[c] = p[c] + enter_west * carry
        carry = ends[c] + r128 * carry
    total = begins[-1]
    for c in range(cols - 2, -1, -1):
        total = begins[c] + r128 * total
    carry = closed(total, -1)
    for c in range(cols - 1, -1, -1):
        q[c] = q[c] + (enter_tail if c == cols - 1 else enter_east) * carry
        carry = begins[c] + (r_rem if c == cols - 1 else r128) * carry
    return [jnp.where(marked, gain * (p[c] + q[c] - s[c]), s[c]) for c in range(cols)]


def rows_kernel(plan, place, cx, cy, shift, mask, table, x_ref, out_ref, held, joined):
    blocks, pitch, own, cols, lat = plan.blocks, plan.pitch, plan.own, plan.cols, plan.lat
    me = place[0]
    band = place[1]

    def steps(x, t, row):
        return row_steps(
            plan, x, cx[t, row], shift[t, row], mask[0, row] == 1, lambda i: table[i, row], joined
        )

    def first_pass(slot, none):
        x = [
            x_ref[pl.ds(slot * pitch + c, blocks, stride=plan.slots * pitch), :]
            for c in range(cols)
        ]
        flat = me * own + slot - HALO
        south = slot >= own + HALO
        row = jnp.where(south, band * lat + slot - (own + 2 * HALO), band * lat + lax.rem(flat + lat, lat))
        y = steps(x, 0, jnp.maximum(row, 0))
        outside = jnp.logical_and(south, band == 0)
        for c in range(cols):
            held[slot, :, c * LANES : (c + 1) * LANES] = jnp.where(outside, 0.0, y[c])
        return none

    lax.fori_loop(0, plan.slots, first_pass, 0)

    def second_pass(m, none):
        j = lax.rem(me * own + m, lat)
        row = band * lat + j
        s0 = m + HALO
        s1 = jnp.where(j == 0, own + 3, s0 - 1)
        s2 = jnp.where(j == 0, own + 2, jnp.where(j == 1, own + 3, s0 - 2))
        c0 = jnp.where(row == 0, 0.0, cy[0, row])
        c1 = jnp.where(row == plan.lat_total - 1, 0.0, cy[0, jnp.minimum(row + 1, plan.lat_total - 1)])
        h0, h1 = 0.5 * (1.0 - c0), 0.5 * (1.0 - c1)
        a0 = 1.0 - c1 * (1.0 + h1)
        a1 = c1 * h1 + c0 * (1.0 + h0)
        a2 = -c0 * h0
        x = []
        for c in range(cols):
            at = slice(c * LANES, (c + 1) * LANES)
            x.append(a0 * held[s0, :, at] + a1 * held[s1, :, at] + a2 * held[s2, :, at])
        y = steps(x, 1, row)
        for c in range(cols):
            out_ref[pl.ds(m * pitch + c, blocks, stride=own * pitch), :] = y[c]
        return none

    lax.fori_loop(0, own, second_pass, 0)


def back_kernel(plan, coef_ref, x_ref, out_ref, got, got_south, send, recv, south_send, south_recv, own_sem):
    me = lax.axis_index("lon")
    band = lax.axis_index("lat")
    blocks, pitch, own, lat = plan.blocks, plan.pitch, plan.own, plan.lat
    size = own * pitch
    here = pl.multiple_of(me * size, 8)
    pieces = [
        (f, part) for f in range(plan.fields) for part in range(HALO // plan.unit)
    ]

    def south(i, to):
        f, part = pieces[i]
        flat = f * lat + lat - HALO + part * plan.unit
        inside = flat - (flat // own) * own
        return pltpu.make_async_remote_copy(
            src_ref=x_ref.at[to, pl.ds(inside * pitch, plan.unit * pitch)],
            dst_ref=got_south.at[pl.ds((f * HALO + part * plan.unit) * pitch, plan.unit * pitch)],
            send_sem=south_send.at[i, to],
            recv_sem=south_recv.at[i],
            device_id={"lon": jnp.int32(to), "lat": lax.rem(band + 1, plan.bands)},
            device_id_type=MESH,
        )

    def owner(i):
        f, part = pieces[i]
        return (f * lat + lat - HALO + part * plan.unit) // own

    local = pltpu.make_async_copy(x_ref.at[me], got.at[pl.ds(here, size)], own_sem)
    local.start()
    copies = []
    for k in range(1, blocks):
        to = lax.rem(me + k, blocks)
        copy = pltpu.make_async_remote_copy(
            src_ref=x_ref.at[to],
            dst_ref=got.at[pl.ds(here, size)],
            send_sem=send.at[k],
            recv_sem=recv.at[k],
            device_id={"lon": to, "lat": band},
            device_id_type=MESH,
        )
        copy.start()
        copies.append(copy)
    for i in range(len(pieces)):

        @pl.when(jnp.logical_and(band < plan.bands - 1, me == owner(i)))
        def _():
            for to in range(blocks):
                south(i, to).start()

    local.wait()
    for copy in copies:
        copy.wait()
    for i in range(len(pieces)):

        @pl.when(jnp.logical_and(band < plan.bands - 1, me == owner(i)))
        def _():
            for to in range(blocks):
                south(i, to).wait_send()

    @pl.when(band > 0)
    def _():
        for i in range(len(pieces)):
            south(i, 0).wait_recv()

    @pl.when(band == 0)
    def _():
        got_south[...] = jnp.zeros_like(got_south)

    sub = lax.broadcasted_iota(jnp.int32, (8, LANES), 0)

    def one_field(f, none):
        for g in range(lat // 8):
            a0, a1, a2 = (coef_ref[i, g * 8 : g * 8 + 8, :] for i in range(3))
            for c in range(plan.cols):
                base = (f * lat + g * 8) * pitch + c
                x0 = got[pl.ds(base, 8, stride=pitch), :]
                if g:
                    x1 = got[pl.ds(base - pitch, 8, stride=pitch), :]
                    x2 = got[pl.ds(base - 2 * pitch, 8, stride=pitch), :]
                else:
                    south2 = got_south[pl.ds(f * HALO * pitch + c, 1), :]
                    south1 = got_south[pl.ds((f * HALO + 1) * pitch + c, 1), :]
                    x1 = jnp.where(sub == 0, south1, pltpu.roll(x0, 1, 0))
                    x2 = jnp.where(
                        sub == 0, south2, jnp.where(sub == 1, south1, pltpu.roll(x0, 2, 0))
                    )
                v = a0 * x0 + a1 * x1 + a2 * x2
                width = LANES if c < plan.cols - 1 else plan.rem
                out_ref[f, 0, g * 8 : g * 8 + 8, c * LANES : c * LANES + width] = v[:, :width]
        return none

    lax.fori_loop(0, plan.fields, one_field, 0)


def body(plan, fields, frac_x, frac_y, shift_cells, polar_mask):
    blocks, pitch, own, lat = plan.blocks, plan.pitch, plan.own, plan.lat
    me = lax.axis_index("lon")
    band = lax.axis_index("lat")
    vmem = pl.BlockSpec(memory_space=pltpu.VMEM)
    smem = pl.BlockSpec(memory_space=pltpu.SMEM)
    anywhere = pl.BlockSpec(memory_space=pl.ANY)
    dma = pltpu.SemaphoreType.DMA
    spread = pl.pallas_call(
        functools.partial(spread_kernel, plan),
        out_shape=jax.ShapeDtypeStruct((blocks, plan.slots * pitch, LANES), jnp.float32),
        in_specs=[vmem],
        out_specs=anywhere,
        scratch_shapes=[
            pltpu.VMEM(((HALO + plan.rows) * pitch, LANES), jnp.float32),
            dma((blocks,)),
            dma((blocks,)),
            dma((len(plan.south_to),)),
            dma((blocks,)),
            dma,
        ],
        compiler_params=pltpu.CompilerParams(has_side_effects=True, vmem_limit_bytes=VMEM_LIMIT),
        name="to_rows",
    )(fields.reshape(plan.rows, plan.lon))

    place = jnp.stack([me, band]).astype(jnp.int32)
    filtered = pl.pallas_call(
        functools.partial(rows_kernel, plan),
        out_shape=jax.ShapeDtypeStruct((blocks * own * pitch, LANES), jnp.float32),
        in_specs=[smem] * 6 + [vmem],
        out_specs=vmem,
        scratch_shapes=[
            pltpu.VMEM((plan.slots, blocks, plan.cols * LANES), jnp.float32),
            pltpu.VMEM((blocks, 2 * plan.cols * LANES), jnp.float32),
        ],
        compiler_params=pltpu.CompilerParams(vmem_limit_bytes=VMEM_LIMIT),
        name="row_steps",
    )(
        place,
        frac_x[:, 0, :],
        frac_y[:, 0, :],
        shift_cells[:, 0, :],
        polar_mask[None],
        jnp.asarray(decay_table(plan)),
        spread.reshape(blocks * plan.slots * pitch, LANES),
    )

    faces = frac_y[SUBS - 1, 0]
    ids = jnp.arange(plan.lat_total, dtype=jnp.int32)
    c0 = jnp.where(ids == 0, 0.0, faces)
    c1 = jnp.where(ids == plan.lat_total - 1, 0.0, jnp.roll(faces, -1))
    h0, h1 = 0.5 * (1.0 - c0), 0.5 * (1.0 - c1)
    coef = jnp.stack([1.0 - c1 * (1.0 + h1), c1 * h1 + c0 * (1.0 + h0), -c0 * h0])
    coef = lax.dynamic_slice_in_dim(coef, band * lat, lat, 1)
    coef = jnp.broadcast_to(coef[:, :, None], (3, lat, LANES))

    n_pieces = plan.fields * (HALO // plan.unit)
    return pl.pallas_call(
        functools.partial(back_kernel, plan),
        out_shape=jax.ShapeDtypeStruct(fields.shape, jnp.float32),
        in_specs=[vmem, anywhere],
        out_specs=vmem,
        scratch_shapes=[
            pltpu.VMEM((plan.rows * pitch, LANES), jnp.float32),
            pltpu.VMEM((plan.fields * HALO * pitch, LANES), jnp.float32),
            dma((blocks,)),
            dma((blocks,)),
            dma((n_pieces, blocks)),
            dma((n_pieces,)),
            dma,
        ],
        compiler_params=pltpu.CompilerParams(has_side_effects=True, vmem_limit_bytes=VMEM_LIMIT),
        name="to_longitudes",
    )(coef, filtered.reshape(blocks, own * pitch, LANES))


def solution(mesh):
    def whole(fields, frac_x, frac_y, shift_cells, polar_mask):
        return jax.shard_map(
            functools.partial(body, Plan(mesh, fields.shape)),
            mesh=mesh,
            in_specs=(P(None, None, "lat", "lon"), P(), P(), P(), P()),
            out_specs=P(None, None, "lat", "lon"),
            check_vma=False,
        )(fields, frac_x, frac_y, shift_cells, polar_mask)

    return whole
```

```python
import functools
import math

import jax
import jax.numpy as jnp
import numpy as np
from jax import lax
from jax.experimental import pallas as pl
from jax.experimental.pallas import tpu as pltpu
from jax.sharding import PartitionSpec as P

SUBS = 2
LANES = 128
HALO = 2
MESH = pl.DeviceIdType.MESH
VMEM_LIMIT = 48 * 1024 * 1024


class Plan:
    def __init__(self, mesh, fields_shape):
        self.blocks = mesh.shape["lon"]
        self.bands = mesh.shape["lat"]
        self.fields, _, self.lat_total, self.lon_total = fields_shape
        self.lat = self.lat_total // self.bands
        self.lon = self.lon_total // self.blocks
        self.cols = -(-self.lon // LANES)
        self.rem = self.lon - LANES * (self.cols - 1)
        self.rows = self.fields * self.lat
        self.own = self.rows // self.blocks
        pitch = self.cols
        while (self.own * pitch) % 8 or (HALO * pitch) % 8:
            pitch += 1
        self.pitch = pitch
        self.slots = self.own + 2 * HALO
        self.unit = 2 if self.own % 2 == 0 else 1
        assert self.rows % self.blocks == 0 and self.own <= self.lat
        assert self.blocks & (self.blocks - 1) == 0 and self.blocks % 8 == 0 and self.lat % 8 == 0
        self.south_to = [
            (f, d)
            for f in range(self.fields)
            for d in sorted({f * self.lat // self.own, (f * self.lat + 1) // self.own})
        ]


def decay_table(plan):
    rows = np.arange(plan.lat_total, dtype=np.float64)
    phi = math.pi * (rows + 0.5) / plan.lat_total - math.pi / 2
    b = np.cos(phi) / math.sin(math.pi * (plan.lat - 0.5) / plan.lat_total)
    log_r = -2.0 * np.arcsinh(b)
    r = np.exp(log_r)
    lines = [np.exp(log_r * 2**k) for k in range(7)]
    lines += [np.exp(log_r * LANES), np.exp(log_r * plan.rem)]
    lines += [(1 - r) / (1 + r), 1 / (1 - np.exp(log_r * plan.lon_total)), log_r]
    lines += [np.exp(log_r * plan.lon * 2**k) for k in range(plan.blocks.bit_length() - 1)]
    table = np.stack(lines).astype(np.float32)
    return np.where(np.abs(table) < 1.2e-38, np.float32(0), table)


def spread_kernel(plan, x_ref, out_ref, packed, send, recv, south_send, south_recv, own_sem):
    me = lax.axis_index("lon")
    band = lax.axis_index("lat")
    blocks, pitch, own = plan.blocks, plan.pitch, plan.own
    packed[0 : HALO * pitch, :] = jnp.zeros((HALO * pitch, LANES), jnp.float32)

    def fill(group, carry):
        for c in range(plan.cols):
            width = LANES if c < plan.cols - 1 else plan.rem
            v = x_ref[pl.ds(pl.multiple_of(group * 8, 8), 8), c * LANES : c * LANES + width]
            if width < LANES:
                v = jnp.concatenate([v, jnp.zeros((8, LANES - width), jnp.float32)], axis=1)
            packed[pl.ds((group * 8 + HALO) * pitch + c, 8, stride=pitch), :] = v
        return carry

    lax.fori_loop(0, plan.rows // 8, fill, 0)
    main = (own + HALO) * pitch
    mine = pl.multiple_of(me * own * pitch, 8)
    local = pltpu.make_async_copy(
        packed.at[pl.ds(mine, main)], out_ref.at[me, pl.ds(0, main)], own_sem
    )
    local.start()
    copies = []
    for k in range(1, blocks):
        to = lax.rem(me + k, blocks)
        copy = pltpu.make_async_remote_copy(
            src_ref=packed.at[pl.ds(pl.multiple_of(to * own * pitch, 8), main)],
            dst_ref=out_ref.at[me, pl.ds(0, main)],
            send_sem=send.at[k],
            recv_sem=recv.at[k],
            device_id={"lon": to, "lat": band},
            device_id_type=MESH,
        )
        copy.start()
        copies.append(copy)

    def south(i):
        f, d = plan.south_to[i]
        first = (HALO + f * plan.lat + plan.lat - HALO) * pitch
        return pltpu.make_async_remote_copy(
            src_ref=packed.at[pl.ds(first, HALO * pitch)],
            dst_ref=out_ref.at[me, pl.ds(main, HALO * pitch)],
            send_sem=south_send.at[i],
            recv_sem=south_recv.at[me],
            device_id={"lon": jnp.int32(d), "lat": lax.rem(band + 1, plan.bands)},
            device_id_type=MESH,
        )

    @pl.when(band < plan.bands - 1)
    def _():
        for i in range(len(plan.south_to)):
            south(i).start()

    local.wait()
    for copy in copies:
        copy.wait()

    @pl.when(band < plan.bands - 1)
    def _():
        for i in range(len(plan.south_to)):
            south(i).wait_send()

    for d in sorted({d for _, d in plan.south_to}):

        @pl.when(jnp.logical_and(band > 0, me == d))
        def _():
            for source in range(blocks):
                pltpu.make_async_remote_copy(
                    src_ref=packed.at[pl.ds(0, HALO * pitch)],
                    dst_ref=out_ref.at[source, pl.ds(main, HALO * pitch)],
                    send_sem=south_send.at[0],
                    recv_sem=south_recv.at[source],
                    device_id={"lon": me, "lat": band - 1},
                    device_id_type=MESH,
                ).wait_recv()


def build_weights(table, row, weights, slot):
    i = lax.broadcasted_iota(jnp.int32, (LANES, LANES), 0)
    j = lax.broadcasted_iota(jnp.int32, (LANES, LANES), 1)
    apart = jnp.abs(i - j).astype(jnp.float32)
    full = table[9, row] * jnp.exp(table[11, row] * apart)
    high = full.astype(jnp.bfloat16)
    low = (full - high.astype(jnp.float32)).astype(jnp.bfloat16)
    for k in range(2):
        weights[slot, k * LANES : (k + 1) * LANES, :LANES] = high
        weights[slot, k * LANES : (k + 1) * LANES, LANES:] = low


def row_steps(plan, x, courant, count, marked, power, joined, weights):
    blocks, cols, rem = plan.blocks, plan.cols, plan.rem
    lane = lax.broadcasted_iota(jnp.int32, (blocks, LANES), 1)
    tail = lane < rem
    x = x[:-1] + [jnp.where(tail, x[-1], 0.0)]

    half = 0.5 * (1.0 - courant)
    w0 = 1.0 - courant * (1.0 + half)
    w1 = courant * (1.0 + 2.0 * half)
    w2 = -courant * half
    west = pltpu.roll(x[-1], 1, 0)
    before1 = pltpu.roll(west, LANES + 1 - rem, 1) if rem > 1 else west
    before2 = pltpu.roll(west, LANES + 2 - rem, 1)
    zonal = []
    for c in range(cols):
        one, two = pltpu.roll(x[c], 1, 1), pltpu.roll(x[c], 2, 1)
        zonal.append(
            w0 * x[c]
            + w1 * jnp.where(lane < 1, before1, one)
            + w2 * jnp.where(lane < 2, before2, two)
        )
        before1, before2 = one, two

    count = jnp.where(count < 0, count + plan.lon_total, count)
    jump = count // plan.lon
    start = plan.lon - (count - jump * plan.lon)
    moved = [pltpu.roll(z, jump, 0) for z in zonal]
    western = [pltpu.roll(m, 1, 0) for m in moved]
    turned = [pltpu.roll(m, rem % LANES, 1) for m in moved]
    for c in range(cols - 1):
        joined[:, c * LANES : (c + 1) * LANES] = western[c]
    for c in range(cols + 1):
        left = western[-1] if c == 0 else turned[c - 1]
        right = turned[c] if c < cols else left
        at = (cols - 1 + c) * LANES
        joined[:, at : at + LANES] = jnp.where(tail, left, right)
    first = start // LANES
    within = start - first * LANES
    window = [
        joined[:, pl.ds(pl.multiple_of((first + c) * LANES, LANES), LANES)] for c in range(cols + 1)
    ]
    window = [pltpu.roll(w, lax.rem(LANES - within, LANES), 1) for w in window]
    keep = lane < LANES - within
    s = [jnp.where(keep, window[c], window[c + 1]) for c in range(cols)]
    s[-1] = jnp.where(tail, s[-1], 0.0)

    r128, r_rem = power(7), power(8)
    closing, log_r = power(10), power(11)
    lane_f = lane.astype(jnp.float32)
    enter_west = jnp.exp(log_r * (lane_f + 1.0))
    enter_east = jnp.exp(log_r * (LANES - lane_f))
    enter_tail = jnp.exp(log_r * jnp.maximum(rem - lane_f, 0.0))
    stacked = jnp.concatenate(s, axis=0)
    high = stacked.astype(jnp.bfloat16)
    low = (stacked - high.astype(jnp.float32)).astype(jnp.bfloat16)
    product = jnp.dot(
        jnp.concatenate([high, low], axis=1), weights, preferred_element_type=jnp.float32
    )
    product = product[:, :LANES] + product[:, LANES:]
    y = [product[c * blocks : (c + 1) * blocks] for c in range(cols)]

    def spread(column, at):
        return jnp.broadcast_to(column[:, at : at + 1], (blocks, LANES))

    ends = [spread(y[c], LANES - 1 if c < cols - 1 else rem - 1) for c in range(cols)]
    begins = [spread(y[c], 0) for c in range(cols)]

    def closed(total, sign):
        total = pltpu.roll(total, 1 if sign > 0 else blocks - 1, 0)
        for k in range(blocks.bit_length() - 1):
            by = 1 << k
            total = total + power(12 + k) * pltpu.roll(total, by if sign > 0 else blocks - by, 0)
        return total * closing

    total = ends[0]
    for c in range(1, cols):
        total = ends[c] + (r128 if c < cols - 1 else r_rem) * total
    carry = closed(total, 1)
    for c in range(cols):
        y[c] = y[c] + enter_west * carry
        carry = ends[c] + r128 * carry
    total = begins[-1]
    for c in range(cols - 2, -1, -1):
        total = begins[c] + r128 * total
    carry = closed(total, -1)
    for c in range(cols - 1, -1, -1):
        y[c] = y[c] + (enter_tail if c == cols - 1 else enter_east) * carry
        carry = begins[c] + (r_rem if c == cols - 1 else r128) * carry
    return [jnp.where(marked, y[c], s[c]) for c in range(cols)]


def face_weights(plan, cy, t, row):
    last = plan.lat_total - 1
    c0 = jnp.where(row == 0, 0.0, cy[t, 0, row])
    c1 = jnp.where(row == last, 0.0, cy[t, 0, jnp.minimum(row + 1, last)])
    h0, h1 = 0.5 * (1.0 - c0), 0.5 * (1.0 - c1)
    return 1.0 - c1 * (1.0 + h1), c1 * h1 + c0 * (1.0 + h0), -c0 * h0


def rows_kernel(plan, cx, cy, shift, mask, table, x_ref, out_ref, held, weights, *joined):
    blocks, pitch, own, cols, lat = plan.blocks, plan.pitch, plan.own, plan.cols, plan.lat
    me = lax.axis_index("lon")
    band = lax.axis_index("lat")

    def steps(x, t, row, slot, part):
        return row_steps(
            plan,
            x,
            cx[t, 0, row],
            shift[t, 0, row],
            mask[row] == 1,
            lambda i: table[i, row],
            joined[part],
            weights[slot],
        )

    def place(slot):
        flat = me * own + slot - HALO
        south = slot >= own + HALO
        row = jnp.where(south, slot - (own + 2 * HALO), lax.rem(flat + lat, lat))
        return south, jnp.maximum(band * lat + row, 0)

    def build(slot, none):
        build_weights(table, place(slot)[1], weights, slot)
        return none

    lax.fori_loop(0, plan.slots, build, 0)

    def first_pass(slot, part):
        south, row = place(slot)
        x = [
            x_ref[pl.ds(slot * pitch + c, blocks, stride=plan.slots * pitch), :]
            for c in range(cols)
        ]
        y = steps(x, 0, row, slot, part)
        outside = jnp.logical_and(south, band == 0)
        for c in range(cols):
            held[slot, :, c * LANES : (c + 1) * LANES] = jnp.where(outside, 0.0, y[c])

    def second_pass(m, part):
        j = lax.rem(me * own + m, lat)
        row = band * lat + j
        s0 = m + HALO
        s1 = jnp.where(j == 0, own + 3, s0 - 1)
        s2 = jnp.where(j == 0, own + 2, jnp.where(j == 1, own + 3, s0 - 2))
        a0, a1, a2 = face_weights(plan, cy, 0, row)
        x = []
        for c in range(cols):
            at = slice(c * LANES, (c + 1) * LANES)
            x.append(a0 * held[s0, :, at] + a1 * held[s1, :, at] + a2 * held[s2, :, at])
        y = steps(x, 1, row, s0, part)
        for c in range(cols):
            out_ref[pl.ds(m * pitch + c, blocks, stride=own * pitch), :] = y[c]

    def loop(count, each):
        width = 2 if count % 2 == 0 else 1

        def step(i, none):
            for part in range(width):
                each(i * width + part, part)
            return none

        lax.fori_loop(0, count // width, step, 0)

    loop(plan.slots, first_pass)
    loop(own, second_pass)


def back_kernel(plan, cy, x_ref, out_ref, coef_ref, got, got_south, send, recv, south_send, south_recv, own_sem):
    me = lax.axis_index("lon")
    band = lax.axis_index("lat")
    blocks, pitch, own, lat = plan.blocks, plan.pitch, plan.own, plan.lat
    size = own * pitch
    here = pl.multiple_of(me * size, 8)
    pieces = [
        (f, part) for f in range(plan.fields) for part in range(HALO // plan.unit)
    ]

    def south(i, to):
        f, part = pieces[i]
        flat = f * lat + lat - HALO + part * plan.unit
        inside = flat - (flat // own) * own
        return pltpu.make_async_remote_copy(
            src_ref=x_ref.at[to, pl.ds(inside * pitch, plan.unit * pitch)],
            dst_ref=got_south.at[pl.ds((f * HALO + part * plan.unit) * pitch, plan.unit * pitch)],
            send_sem=south_send.at[i, to],
            recv_sem=south_recv.at[i],
            device_id={"lon": jnp.int32(to), "lat": lax.rem(band + 1, plan.bands)},
            device_id_type=MESH,
        )

    def owner(i):
        f, part = pieces[i]
        return (f * lat + lat - HALO + part * plan.unit) // own

    local = pltpu.make_async_copy(x_ref.at[me], got.at[pl.ds(here, size)], own_sem)
    local.start()
    copies = []
    for k in range(1, blocks):
        to = lax.rem(me + k, blocks)
        copy = pltpu.make_async_remote_copy(
            src_ref=x_ref.at[to],
            dst_ref=got.at[pl.ds(here, size)],
            send_sem=send.at[k],
            recv_sem=recv.at[k],
            device_id={"lon": to, "lat": band},
            device_id_type=MESH,
        )
        copy.start()
        copies.append(copy)
    for i in range(len(pieces)):

        @pl.when(jnp.logical_and(band < plan.bands - 1, me == owner(i)))
        def _():
            for to in range(blocks):
                south(i, to).start()

    for j in range(lat):
        for i, weight in enumerate(face_weights(plan, cy, SUBS - 1, band * lat + j)):
            coef_ref[i, j : j + 1, :] = jnp.full((1, LANES), weight, jnp.float32)

    local.wait()
    for copy in copies:
        copy.wait()
    for i in range(len(pieces)):

        @pl.when(jnp.logical_and(band < plan.bands - 1, me == owner(i)))
        def _():
            for to in range(blocks):
                south(i, to).wait_send()

    @pl.when(band > 0)
    def _():
        for i in range(len(pieces)):
            south(i, 0).wait_recv()

    @pl.when(band == 0)
    def _():
        got_south[...] = jnp.zeros_like(got_south)

    sub = lax.broadcasted_iota(jnp.int32, (8, LANES), 0)

    def one_field(f, none):
        for g in range(lat // 8):
            a0, a1, a2 = (coef_ref[i, g * 8 : g * 8 + 8, :] for i in range(3))
            for c in range(plan.cols):
                base = (f * lat + g * 8) * pitch + c
                x0 = got[pl.ds(base, 8, stride=pitch), :]
                if g:
                    x1 = got[pl.ds(base - pitch, 8, stride=pitch), :]
                    x2 = got[pl.ds(base - 2 * pitch, 8, stride=pitch), :]
                else:
                    south2 = got_south[pl.ds(f * HALO * pitch + c, 1), :]
                    south1 = got_south[pl.ds((f * HALO + 1) * pitch + c, 1), :]
                    x1 = jnp.where(sub == 0, south1, pltpu.roll(x0, 1, 0))
                    x2 = jnp.where(
                        sub == 0, south2, jnp.where(sub == 1, south1, pltpu.roll(x0, 2, 0))
                    )
                v = a0 * x0 + a1 * x1 + a2 * x2
                width = LANES if c < plan.cols - 1 else plan.rem
                out_ref[f, 0, g * 8 : g * 8 + 8, c * LANES : c * LANES + width] = v[:, :width]
        return none

    lax.fori_loop(0, plan.fields, one_field, 0)


def body(plan, fields, frac_x, frac_y, shift_cells, polar_mask):
    blocks, pitch, own, lat = plan.blocks, plan.pitch, plan.own, plan.lat
    vmem = pl.BlockSpec(memory_space=pltpu.VMEM)
    smem = pl.BlockSpec(memory_space=pltpu.SMEM)
    anywhere = pl.BlockSpec(memory_space=pl.ANY)
    dma = pltpu.SemaphoreType.DMA
    spread = pl.pallas_call(
        functools.partial(spread_kernel, plan),
        out_shape=jax.ShapeDtypeStruct((blocks, plan.slots * pitch, LANES), jnp.float32),
        in_specs=[vmem],
        out_specs=anywhere,
        scratch_shapes=[
            pltpu.VMEM(((HALO + plan.rows) * pitch, LANES), jnp.float32),
            dma((blocks,)),
            dma((blocks,)),
            dma((len(plan.south_to),)),
            dma((blocks,)),
            dma,
        ],
        compiler_params=pltpu.CompilerParams(has_side_effects=True, vmem_limit_bytes=VMEM_LIMIT),
        name="to_rows",
    )(fields.reshape(plan.rows, plan.lon))

    filtered = pl.pallas_call(
        functools.partial(rows_kernel, plan),
        out_shape=jax.ShapeDtypeStruct((blocks * own * pitch, LANES), jnp.float32),
        in_specs=[smem] * 5 + [vmem],
        out_specs=vmem,
        scratch_shapes=[
            pltpu.VMEM((plan.slots, blocks, plan.cols * LANES), jnp.float32),
            pltpu.VMEM((plan.slots, 2 * LANES, 2 * LANES), jnp.bfloat16),
            pltpu.VMEM((blocks, 2 * plan.cols * LANES), jnp.float32),
            pltpu.VMEM((blocks, 2 * plan.cols * LANES), jnp.float32),
        ],
        compiler_params=pltpu.CompilerParams(vmem_limit_bytes=VMEM_LIMIT),
        name="row_steps",
    )(
        frac_x,
        frac_y,
        shift_cells,
        polar_mask,
        jnp.asarray(decay_table(plan)),
        spread.reshape(blocks * plan.slots * pitch, LANES),
    )

    n_pieces = plan.fields * (HALO // plan.unit)
    return pl.pallas_call(
        functools.partial(back_kernel, plan),
        out_shape=jax.ShapeDtypeStruct(fields.shape, jnp.float32),
        in_specs=[smem, anywhere],
        out_specs=vmem,
        scratch_shapes=[
            pltpu.VMEM((3, lat, LANES), jnp.float32),
            pltpu.VMEM((plan.rows * pitch, LANES), jnp.float32),
            pltpu.VMEM((plan.fields * HALO * pitch, LANES), jnp.float32),
            dma((blocks,)),
            dma((blocks,)),
            dma((n_pieces, blocks)),
            dma((n_pieces,)),
            dma,
        ],
        compiler_params=pltpu.CompilerParams(has_side_effects=True, vmem_limit_bytes=VMEM_LIMIT),
        name="to_longitudes",
    )(frac_y, filtered.reshape(blocks, own * pitch, LANES))


def solution(mesh):
    def whole(fields, frac_x, frac_y, shift_cells, polar_mask):
        return jax.shard_map(
            functools.partial(body, Plan(mesh, fields.shape)),
            mesh=mesh,
            in_specs=(P(None, None, "lat", "lon"), P(), P(), P(), P()),
            out_specs=P(None, None, "lat", "lon"),
            check_vma=False,
        )(fields, frac_x, frac_y, shift_cells, polar_mask)

    return whole
```

```python
import functools
import math

import jax
import jax.numpy as jnp
import numpy as np
from jax import lax
from jax.experimental import pallas as pl
from jax.experimental.pallas import tpu as pltpu
from jax.sharding import PartitionSpec as P

SUBS = 2
LANES = 128
HALO = 2
MESH = pl.DeviceIdType.MESH
VMEM_LIMIT = 48 * 1024 * 1024


class Plan:
    def __init__(self, mesh, fields_shape):
        self.blocks = mesh.shape["lon"]
        self.bands = mesh.shape["lat"]
        self.fields, _, self.lat_total, self.lon_total = fields_shape
        self.lat = self.lat_total // self.bands
        self.lon = self.lon_total // self.blocks
        self.cols = -(-self.lon // LANES)
        self.rem = self.lon - LANES * (self.cols - 1)
        self.rows = self.fields * self.lat
        self.own = self.rows // self.blocks
        pitch = self.cols
        while (self.own * pitch) % 8 or (HALO * pitch) % 8:
            pitch += 1
        self.pitch = pitch
        self.slots = self.own + 2 * HALO
        self.group = 4 if self.own % 4 == 0 else self.own
        self.groups = self.own // self.group
        self.unit = 2 if self.own % 2 == 0 else 1
        assert self.rows % self.blocks == 0 and self.own <= self.lat
        assert self.blocks & (self.blocks - 1) == 0 and self.blocks % 8 == 0 and self.lat % 8 == 0
        self.south_to = [
            (f, d)
            for f in range(self.fields)
            for d in sorted({f * self.lat // self.own, (f * self.lat + 1) // self.own})
        ]


def decay_table(plan):
    rows = np.arange(plan.lat_total, dtype=np.float64)
    phi = math.pi * (rows + 0.5) / plan.lat_total - math.pi / 2
    b = np.cos(phi) / math.sin(math.pi * (plan.lat - 0.5) / plan.lat_total)
    log_r = -2.0 * np.arcsinh(b)
    r = np.exp(log_r)
    lines = [np.exp(log_r * 2**k) for k in range(7)]
    lines += [np.exp(log_r * LANES), np.exp(log_r * plan.rem)]
    lines += [(1 - r) / (1 + r), 1 / (1 - np.exp(log_r * plan.lon_total)), log_r]
    lines += [np.exp(log_r * plan.lon * 2**k) for k in range(plan.blocks.bit_length() - 1)]
    table = np.stack(lines).astype(np.float32)
    return np.where(np.abs(table) < 1.2e-38, np.float32(0), table)


def build_weights(table, row, weights, slot):
    i = lax.broadcasted_iota(jnp.int32, (LANES, LANES), 0)
    j = lax.broadcasted_iota(jnp.int32, (LANES, LANES), 1)
    apart = jnp.abs(i - j).astype(jnp.float32)
    full = table[9, row] * jnp.exp(table[11, row] * apart)
    high = full.astype(jnp.bfloat16)
    low = (full - high.astype(jnp.float32)).astype(jnp.bfloat16)
    for k in range(2):
        weights[slot, k * LANES : (k + 1) * LANES, :LANES] = high
        weights[slot, k * LANES : (k + 1) * LANES, LANES:] = low


def row_steps(plan, x, courant, count, marked, power, weights):
    blocks, cols, rem = plan.blocks, plan.cols, plan.rem
    lane = lax.broadcasted_iota(jnp.int32, (blocks, LANES), 1)
    tail = lane < rem
    x = x[:-1] + [jnp.where(tail, x[-1], 0.0)]

    half = 0.5 * (1.0 - courant)
    w0 = 1.0 - courant * (1.0 + half)
    w1 = courant * (1.0 + 2.0 * half)
    w2 = -courant * half
    west = pltpu.roll(x[-1], 1, 0)
    before1 = pltpu.roll(west, LANES + 1 - rem, 1) if rem > 1 else west
    before2 = pltpu.roll(west, LANES + 2 - rem, 1)
    zonal = []
    for c in range(cols):
        one, two = pltpu.roll(x[c], 1, 1), pltpu.roll(x[c], 2, 1)
        zonal.append(
            w0 * x[c]
            + w1 * jnp.where(lane < 1, before1, one)
            + w2 * jnp.where(lane < 2, before2, two)
        )
        before1, before2 = one, two

    count = lax.rem(count + plan.lon_total, plan.lon_total)
    moved = [pltpu.roll(z, lax.div(count, plan.lon), 0) for z in zonal]
    start = plan.lon - lax.rem(count, plan.lon)
    western = [pltpu.roll(m, 1, 0) for m in moved]
    turned = [pltpu.roll(m, rem % LANES, 1) for m in moved]
    window = western[:-1]
    for c in range(cols + 1):
        left = western[-1] if c == 0 else turned[c - 1]
        right = turned[c] if c < cols else left
        window.append(jnp.where(tail, left, right))
    first = jnp.full((blocks, LANES), start, jnp.int32) >> 7
    for k in reversed(range((cols - 1).bit_length())):
        by = 1 << k
        taken = (first & by) == by
        window = [
            jnp.where(taken, window[i + by], window[i]) if i + by < len(window) else window[i]
            for i in range(min(len(window), cols + by))
        ]
    within = start & (LANES - 1)
    window = [pltpu.roll(w, (LANES - within) & (LANES - 1), 1) for w in window]
    keep = lane < LANES - jnp.full((blocks, LANES), within, jnp.int32)
    s = [jnp.where(keep, window[c], window[c + 1]) for c in range(cols)]
    s[-1] = jnp.where(tail, s[-1], 0.0)

    r128, r_rem = power(7), power(8)
    closing, log_r = power(10), power(11)
    lane_f = lane.astype(jnp.float32)
    enter_west = jnp.exp(log_r * (lane_f + 1.0))
    enter_east = jnp.exp(log_r * (LANES - lane_f))
    enter_tail = jnp.exp(log_r * jnp.maximum(rem - lane_f, 0.0))
    stacked = jnp.concatenate(s, axis=0)
    high = stacked.astype(jnp.bfloat16)
    low = (stacked - high.astype(jnp.float32)).astype(jnp.bfloat16)
    product = jnp.dot(
        jnp.concatenate([high, low], axis=1), weights, preferred_element_type=jnp.float32
    )
    product = product[:, :LANES] + product[:, LANES:]
    y = [product[c * blocks : (c + 1) * blocks] for c in range(cols)]

    def spread(column, at):
        return jnp.broadcast_to(column[:, at : at + 1], (blocks, LANES))

    ends = [spread(y[c], LANES - 1 if c < cols - 1 else rem - 1) for c in range(cols)]
    begins = [spread(y[c], 0) for c in range(cols)]

    def closed(total, sign):
        total = pltpu.roll(total, 1 if sign > 0 else blocks - 1, 0)
        for k in range(blocks.bit_length() - 1):
            by = 1 << k
            total = total + power(12 + k) * pltpu.roll(total, by if sign > 0 else blocks - by, 0)
        return total * closing

    total = ends[0]
    for c in range(1, cols):
        total = ends[c] + (r128 if c < cols - 1 else r_rem) * total
    carry = closed(total, 1)
    for c in range(cols):
        y[c] = y[c] + enter_west * carry
        carry = ends[c] + r128 * carry
    total = begins[-1]
    for c in range(cols - 2, -1, -1):
        total = begins[c] + r128 * total
    carry = closed(total, -1)
    for c in range(cols - 1, -1, -1):
        y[c] = y[c] + (enter_tail if c == cols - 1 else enter_east) * carry
        carry = begins[c] + (r_rem if c == cols - 1 else r128) * carry
    filtered = jnp.full((blocks, LANES), marked, jnp.int32) == 1
    return [jnp.where(filtered, y[c], s[c]) for c in range(cols)]


def face_weights(plan, cy, t, row):
    last = plan.lat_total - 1
    c0 = jnp.where(row == 0, 0.0, cy[t, 0, row])
    c1 = jnp.where(row == last, 0.0, cy[t, 0, jnp.minimum(row + 1, last)])
    h0, h1 = 0.5 * (1.0 - c0), 0.5 * (1.0 - c1)
    return 1.0 - c1 * (1.0 + h1), c1 * h1 + c0 * (1.0 + h0), -c0 * h0


def start_all(copies):
    for copy in copies:
        copy.start()


def kernel(
    plan, cx, cy, shift, mask, table, x_ref, out_ref,
    packed, arrived, held, weights, ready, got, got_south, coef,
    in_send, in_recv, halo_send, halo_recv, south_in_send, south_in_recv,
    out_send, out_recv, own_out, south_out_send, south_out_recv, own_in,
):
    blocks, pitch, own, cols, lat = plan.blocks, plan.pitch, plan.own, plan.cols, plan.lat
    group, groups, slots = plan.group, plan.groups, plan.slots
    me = lax.axis_index("lon")
    band = lax.axis_index("lat")
    has_north = band < plan.bands - 1
    north = lax.rem(band + 1, plan.bands)

    def lines(first, count):
        return pl.ds(pl.multiple_of(first * pitch, 8), count * pitch)

    packed[0 : HALO * pitch, :] = jnp.zeros((HALO * pitch, LANES), jnp.float32)

    def fill(part, none):
        for c in range(cols):
            width = LANES if c < cols - 1 else plan.rem
            v = x_ref[pl.ds(pl.multiple_of(part * 8, 8), 8), c * LANES : c * LANES + width]
            if width < LANES:
                v = jnp.concatenate([v, jnp.zeros((8, LANES - width), jnp.float32)], axis=1)
            packed[pl.ds((part * 8 + HALO) * pitch + c, 8, stride=pitch), :] = v
        return none

    lax.fori_loop(0, plan.rows // 8, fill, 0)

    def peer(k):
        return lax.rem(me + k, blocks)

    def halo_in(k):
        return pltpu.make_async_remote_copy(
            src_ref=packed.at[lines(peer(k) * own, HALO)],
            dst_ref=arrived.at[lines(me * slots, HALO)],
            send_sem=halo_send.at[k],
            recv_sem=halo_recv.at[k],
            device_id={"lon": peer(k), "lat": band},
            device_id_type=MESH,
        )

    def group_in(k, g):
        return pltpu.make_async_remote_copy(
            src_ref=packed.at[lines(peer(k) * own + HALO + g * group, group)],
            dst_ref=arrived.at[lines(me * slots + HALO + g * group, group)],
            send_sem=in_send.at[k, g],
            recv_sem=in_recv.at[k, g],
            device_id={"lon": peer(k), "lat": band},
            device_id_type=MESH,
        )

    def south_in(i):
        f, d = plan.south_to[i]
        return pltpu.make_async_remote_copy(
            src_ref=packed.at[lines(HALO + f * lat + lat - HALO, HALO)],
            dst_ref=arrived.at[lines(me * slots + own + HALO, HALO)],
            send_sem=south_in_send.at[i],
            recv_sem=south_in_recv.at[me],
            device_id={"lon": jnp.int32(d), "lat": north},
            device_id_type=MESH,
        )

    local = pltpu.make_async_copy(
        packed.at[lines(me * own, own + HALO)], arrived.at[lines(me * slots, own + HALO)], own_in
    )
    local.start()
    start_all([halo_in(k) for k in range(1, blocks)])

    @pl.when(has_north)
    def _():
        start_all([south_in(i) for i in range(len(plan.south_to))])

    for g in range(groups):
        start_all([group_in(k, g) for k in range(1, blocks)])

    def place(slot):
        flat = me * own + slot - HALO
        south = slot >= own + HALO
        row = jnp.where(south, slot - (own + 2 * HALO), lax.rem(flat + lat, lat))
        return south, jnp.maximum(band * lat + row, 0)

    def build(slot, none):
        build_weights(table, place(slot)[1], weights, slot)
        return none

    lax.fori_loop(0, slots, build, 0)
    for j in range(lat):
        for i, weight in enumerate(face_weights(plan, cy, SUBS - 1, band * lat + j)):
            coef[i, j : j + 1, :] = jnp.full((1, LANES), weight, jnp.float32)

    def steps(x, t, row, slot):
        return row_steps(
            plan,
            x,
            cx[t, 0, row],
            shift[t, 0, row],
            mask[row],
            lambda i: table[i, row],
            weights[slot],
        )

    def first_pass(slot):
        south, row = place(slot)
        x = [arrived[pl.ds(slot * pitch + c, blocks, stride=slots * pitch), :] for c in range(cols)]
        y = steps(x, 0, row, slot)
        outside = jnp.logical_and(south, band == 0)
        for c in range(cols):
            held[slot, :, c * LANES : (c + 1) * LANES] = jnp.where(outside, 0.0, y[c])

    def second_pass(m):
        j = lax.rem(me * own + m, lat)
        row = band * lat + j
        s0 = m + HALO
        s1 = jnp.where(j == 0, own + 3, s0 - 1)
        s2 = jnp.where(j == 0, own + 2, jnp.where(j == 1, own + 3, s0 - 2))
        a0, a1, a2 = face_weights(plan, cy, 0, row)
        x = []
        for c in range(cols):
            at = slice(c * LANES, (c + 1) * LANES)
            x.append(a0 * held[s0, :, at] + a1 * held[s1, :, at] + a2 * held[s2, :, at])
        y = steps(x, 1, row, s0)
        for c in range(cols):
            ready[pl.ds(m * pitch + c, blocks, stride=own * pitch), :] = y[c]

    def loop(count, each):
        width = 2 if count % 2 == 0 else 1

        def step(i, none):
            for part in range(width):
                each(i * width + part)
            return none

        lax.fori_loop(0, count // width, step, 0)

    def own_back(g):
        return pltpu.make_async_copy(
            ready.at[lines(me * own + g * group, group)],
            got.at[lines(me * own + g * group, group)],
            own_out.at[g],
        )

    def group_back(k, g):
        return pltpu.make_async_remote_copy(
            src_ref=ready.at[lines(peer(k) * own + g * group, group)],
            dst_ref=got.at[lines(me * own + g * group, group)],
            send_sem=out_send.at[k, g],
            recv_sem=out_recv.at[k, g],
            device_id={"lon": peer(k), "lat": band},
            device_id_type=MESH,
        )

    pieces = [(f, part) for f in range(plan.fields) for part in range(HALO // plan.unit)]

    def piece_row(i):
        f, part = pieces[i]
        return f * lat + lat - HALO + part * plan.unit

    def south_back(i, to):
        f, part = pieces[i]
        inside = piece_row(i) % own
        return pltpu.make_async_remote_copy(
            src_ref=ready.at[lines(to * own + inside, plan.unit)],
            dst_ref=got_south.at[lines(f * HALO + part * plan.unit, plan.unit)],
            send_sem=south_out_send.at[i, to],
            recv_sem=south_out_recv.at[i],
            device_id={"lon": jnp.int32(to), "lat": north},
            device_id_type=MESH,
        )

    def sends_south(i):
        return jnp.logical_and(has_north, me == piece_row(i) // own)

    local.wait()
    for k in range(1, blocks):
        halo_in(k).wait_recv()
    for d in sorted({d for _, d in plan.south_to}):

        @pl.when(jnp.logical_and(band > 0, me == d))
        def _():
            for source in range(blocks):
                pltpu.make_async_remote_copy(
                    src_ref=packed.at[lines(0, HALO)],
                    dst_ref=arrived.at[lines(source * slots + own + HALO, HALO)],
                    send_sem=south_in_send.at[0],
                    recv_sem=south_in_recv.at[source],
                    device_id={"lon": me, "lat": lax.rem(band + plan.bands - 1, plan.bands)},
                    device_id_type=MESH,
                ).wait_recv()

    loop(2 * HALO, lambda i: first_pass(jnp.where(i < HALO, i, i + own)))

    def one_group(g, none):
        for k in range(1, blocks):
            group_in(k, g).wait_recv()
        loop(group, lambda i: first_pass(HALO + g * group + i))
        loop(group, lambda i: second_pass(g * group + i))
        own_back(g).start()
        start_all([group_back(k, g) for k in range(1, blocks)])
        for i in range(len(pieces)):

            @pl.when(jnp.logical_and(sends_south(i), g == piece_row(i) % own // group))
            def _():
                start_all([south_back(i, to) for to in range(blocks)])

        return none

    lax.fori_loop(0, groups, one_group, 0)

    for k in range(1, blocks):
        halo_in(k).wait_send()
        for g in range(groups):
            group_in(k, g).wait_send()

    @pl.when(has_north)
    def _():
        for i in range(len(plan.south_to)):
            south_in(i).wait_send()

    for g in range(groups):
        own_back(g).wait()
        for k in range(1, blocks):
            group_back(k, g).wait()
    for i in range(len(pieces)):

        @pl.when(sends_south(i))
        def _():
            for to in range(blocks):
                south_back(i, to).wait_send()

    @pl.when(band > 0)
    def _():
        for i in range(len(pieces)):
            south_back(i, 0).wait_recv()

    @pl.when(band == 0)
    def _():
        got_south[...] = jnp.zeros_like(got_south)

    sub = lax.broadcasted_iota(jnp.int32, (8, LANES), 0)

    def one_field(f, none):
        for g in range(lat // 8):
            a0, a1, a2 = (coef[i, g * 8 : g * 8 + 8, :] for i in range(3))
            for c in range(cols):
                base = (f * lat + g * 8) * pitch + c
                x0 = got[pl.ds(base, 8, stride=pitch), :]
                if g:
                    x1 = got[pl.ds(base - pitch, 8, stride=pitch), :]
                    x2 = got[pl.ds(base - 2 * pitch, 8, stride=pitch), :]
                else:
                    south2 = got_south[pl.ds(f * HALO * pitch + c, 1), :]
                    south1 = got_south[pl.ds((f * HALO + 1) * pitch + c, 1), :]
                    x1 = jnp.where(sub == 0, south1, pltpu.roll(x0, 1, 0))
                    x2 = jnp.where(
                        sub == 0, south2, jnp.where(sub == 1, south1, pltpu.roll(x0, 2, 0))
                    )
                v = a0 * x0 + a1 * x1 + a2 * x2
                width = LANES if c < cols - 1 else plan.rem
                out_ref[f, 0, g * 8 : g * 8 + 8, c * LANES : c * LANES + width] = v[:, :width]
        return none

    lax.fori_loop(0, plan.fields, one_field, 0)


def body(plan, fields, frac_x, frac_y, shift_cells, polar_mask):
    blocks, pitch, own, lat = plan.blocks, plan.pitch, plan.own, plan.lat
    vmem = pl.BlockSpec(memory_space=pltpu.VMEM)
    smem = pl.BlockSpec(memory_space=pltpu.SMEM)
    dma = pltpu.SemaphoreType.DMA
    n_pieces = plan.fields * (HALO // plan.unit)

    def lines(rows):
        return pltpu.VMEM((rows * pitch, LANES), jnp.float32)

    return pl.pallas_call(
        functools.partial(kernel, plan),
        out_shape=jax.ShapeDtypeStruct(fields.shape, jnp.float32),
        in_specs=[smem] * 5 + [vmem],
        out_specs=vmem,
        scratch_shapes=[
            lines(HALO + plan.rows),
            lines(blocks * plan.slots),
            pltpu.VMEM((plan.slots, blocks, plan.cols * LANES), jnp.float32),
            pltpu.VMEM((plan.slots, 2 * LANES, 2 * LANES), jnp.bfloat16),
            lines(blocks * own),
            lines(plan.rows),
            lines(plan.fields * HALO),
            pltpu.VMEM((3, lat, LANES), jnp.float32),
            dma((blocks, plan.groups)),
            dma((blocks, plan.groups)),
            dma((blocks,)),
            dma((blocks,)),
            dma((len(plan.south_to),)),
            dma((blocks,)),
            dma((blocks, plan.groups)),
            dma((blocks, plan.groups)),
            dma((plan.groups,)),
            dma((n_pieces, blocks)),
            dma((n_pieces,)),
            dma,
        ],
        compiler_params=pltpu.CompilerParams(has_side_effects=True, vmem_limit_bytes=VMEM_LIMIT),
        name="transport",
    )(
        frac_x,
        frac_y,
        shift_cells,
        polar_mask,
        jnp.asarray(decay_table(plan)),
        fields.reshape(plan.rows, plan.lon),
    )


def solution(mesh):
    def whole(fields, frac_x, frac_y, shift_cells, polar_mask):
        return jax.shard_map(
            functools.partial(body, Plan(mesh, fields.shape)),
            mesh=mesh,
            in_specs=(P(None, None, "lat", "lon"), P(), P(), P(), P()),
            out_specs=P(None, None, "lat", "lon"),
            check_vma=False,
        )(fields, frac_x, frac_y, shift_cells, polar_mask)

    return whole
```

```python
import functools
import math

import jax
import jax.numpy as jnp
import numpy as np
from jax import lax
from jax.experimental import pallas as pl
from jax.experimental.pallas import tpu as pltpu
from jax.sharding import PartitionSpec as P

SUBS = 2
LANES = 128
HALO = 2
MESH = pl.DeviceIdType.MESH
VMEM_LIMIT = 62 * 1024 * 1024


class Plan:
    def __init__(self, mesh, fields_shape):
        self.blocks = mesh.shape["lon"]
        self.bands = mesh.shape["lat"]
        self.fields, _, self.lat_total, self.lon_total = fields_shape
        self.lat = self.lat_total // self.bands
        self.lon = self.lon_total // self.blocks
        self.cols = -(-self.lon // LANES)
        self.rem = self.lon - LANES * (self.cols - 1)
        self.rows = self.fields * self.lat
        self.own = self.rows // self.blocks
        pitch = self.cols
        while (self.own * pitch) % 8 or (HALO * pitch) % 8:
            pitch += 1
        self.pitch = pitch
        self.slots = self.own + 2 * HALO
        self.group = 4 if self.own % 4 == 0 else self.own
        self.groups = self.own // self.group
        self.unit = 2 if self.own % 2 == 0 else 1
        assert self.rows % self.blocks == 0 and self.own <= self.lat
        assert self.blocks & (self.blocks - 1) == 0 and self.blocks % 8 == 0 and self.lat % 8 == 0
        self.south_to = [
            (f, d)
            for f in range(self.fields)
            for d in sorted({f * self.lat // self.own, (f * self.lat + 1) // self.own})
        ]


def decay_table(plan):
    rows = np.arange(plan.lat_total, dtype=np.float64)
    phi = math.pi * (rows + 0.5) / plan.lat_total - math.pi / 2
    b = np.cos(phi) / math.sin(math.pi * (plan.lat - 0.5) / plan.lat_total)
    log_r = -2.0 * np.arcsinh(b)
    r = np.exp(log_r)
    lines = [np.exp(log_r * 2**k) for k in range(7)]
    lines += [np.exp(log_r * LANES), np.exp(log_r * plan.rem)]
    lines += [(1 - r) / (1 + r), 1 / (1 - np.exp(log_r * plan.lon_total)), log_r]
    lines += [np.exp(log_r * plan.lon * 2**k) for k in range(plan.blocks.bit_length() - 1)]
    table = np.stack(lines).astype(np.float32)
    return np.where(np.abs(table) < 1.2e-38, np.float32(0), table)


def build_weights(table, row, weights, slot):
    i = lax.broadcasted_iota(jnp.int32, (LANES, LANES), 0)
    j = lax.broadcasted_iota(jnp.int32, (LANES, LANES), 1)
    apart = jnp.abs(i - j).astype(jnp.float32)
    full = table[9, row] * jnp.exp(table[11, row] * apart)
    high = full.astype(jnp.bfloat16)
    low = (full - high.astype(jnp.float32)).astype(jnp.bfloat16)
    for k in range(2):
        weights[slot, k * LANES : (k + 1) * LANES, :LANES] = high
        weights[slot, k * LANES : (k + 1) * LANES, LANES:] = low


def row_steps(plan, x, courant, count, marked, power, weights):
    blocks, cols, rem = plan.blocks, plan.cols, plan.rem
    lane = lax.broadcasted_iota(jnp.int32, (blocks, LANES), 1)
    tail = lane < rem
    x = x[:-1] + [jnp.where(tail, x[-1], 0.0)]

    half = 0.5 * (1.0 - courant)
    w0 = 1.0 - courant * (1.0 + half)
    w1 = courant * (1.0 + 2.0 * half)
    w2 = -courant * half
    west = pltpu.roll(x[-1], 1, 0)
    before1 = pltpu.roll(west, LANES + 1 - rem, 1) if rem > 1 else west
    before2 = pltpu.roll(west, LANES + 2 - rem, 1)
    zonal = []
    for c in range(cols):
        one, two = pltpu.roll(x[c], 1, 1), pltpu.roll(x[c], 2, 1)
        zonal.append(
            w0 * x[c]
            + w1 * jnp.where(lane < 1, before1, one)
            + w2 * jnp.where(lane < 2, before2, two)
        )
        before1, before2 = one, two

    count = lax.rem(count + plan.lon_total, plan.lon_total)
    moved = [pltpu.roll(z, lax.div(count, plan.lon), 0) for z in zonal]
    start = plan.lon - lax.rem(count, plan.lon)
    western = [pltpu.roll(m, 1, 0) for m in moved]
    turned = [pltpu.roll(m, rem % LANES, 1) for m in moved]
    window = western[:-1]
    for c in range(cols + 1):
        left = western[-1] if c == 0 else turned[c - 1]
        right = turned[c] if c < cols else left
        window.append(jnp.where(tail, left, right))
    first = jnp.full((blocks, LANES), start, jnp.int32) >> 7
    for k in reversed(range((cols - 1).bit_length())):
        by = 1 << k
        taken = (first & by) == by
        window = [
            jnp.where(taken, window[i + by], window[i]) if i + by < len(window) else window[i]
            for i in range(min(len(window), cols + by))
        ]
    within = start & (LANES - 1)
    window = [pltpu.roll(w, (LANES - within) & (LANES - 1), 1) for w in window]
    keep = lane < LANES - jnp.full((blocks, LANES), within, jnp.int32)
    s = [jnp.where(keep, window[c], window[c + 1]) for c in range(cols)]
    s[-1] = jnp.where(tail, s[-1], 0.0)

    r128, r_rem = power(7), power(8)
    closing, log_r = power(10), power(11)
    lane_f = lane.astype(jnp.float32)
    enter_west = jnp.exp(log_r * (lane_f + 1.0))
    enter_east = jnp.exp(log_r * (LANES - lane_f))
    enter_tail = jnp.exp(log_r * jnp.maximum(rem - lane_f, 0.0))
    stacked = jnp.concatenate(s, axis=0)
    high = stacked.astype(jnp.bfloat16)
    low = (stacked - high.astype(jnp.float32)).astype(jnp.bfloat16)
    product = jnp.dot(
        jnp.concatenate([high, low], axis=1), weights, preferred_element_type=jnp.float32
    )
    product = product[:, :LANES] + product[:, LANES:]
    y = [product[c * blocks : (c + 1) * blocks] for c in range(cols)]

    def spread(column, at):
        return jnp.broadcast_to(column[:, at : at + 1], (blocks, LANES))

    ends = [spread(y[c], LANES - 1 if c < cols - 1 else rem - 1) for c in range(cols)]
    begins = [spread(y[c], 0) for c in range(cols)]

    def closed(total, sign):
        total = pltpu.roll(total, 1 if sign > 0 else blocks - 1, 0)
        for k in range(blocks.bit_length() - 1):
            by = 1 << k
            total = total + power(12 + k) * pltpu.roll(total, by if sign > 0 else blocks - by, 0)
        return total * closing

    total = ends[0]
    for c in range(1, cols):
        total = ends[c] + (r128 if c < cols - 1 else r_rem) * total
    carry = closed(total, 1)
    for c in range(cols):
        y[c] = y[c] + enter_west * carry
        carry = ends[c] + r128 * carry
    total = begins[-1]
    for c in range(cols - 2, -1, -1):
        total = begins[c] + r128 * total
    carry = closed(total, -1)
    for c in range(cols - 1, -1, -1):
        y[c] = y[c] + (enter_tail if c == cols - 1 else enter_east) * carry
        carry = begins[c] + (r_rem if c == cols - 1 else r128) * carry
    filtered = jnp.full((blocks, LANES), marked, jnp.int32) == 1
    return [jnp.where(filtered, y[c], s[c]) for c in range(cols)]


def face_weights(plan, cy, t, row):
    last = plan.lat_total - 1
    c0 = jnp.where(row == 0, 0.0, cy[t, 0, row])
    c1 = jnp.where(row == last, 0.0, cy[t, 0, jnp.minimum(row + 1, last)])
    h0, h1 = 0.5 * (1.0 - c0), 0.5 * (1.0 - c1)
    return 1.0 - c1 * (1.0 + h1), c1 * h1 + c0 * (1.0 + h0), -c0 * h0


def start_all(copies):
    for copy in copies:
        copy.start()


def kernel(
    plan, *refs,
):
    inputs, (x_ref, out_ref), tables, rest = refs[:5], refs[5:7], refs[7:12], refs[12:]
    cx, cy, shift, mask, table = tables
    (x_local, x_sem, table_sem, packed, arrived, held, weights, ready, got, got_south, coef,
    in_send, in_recv, halo_send, halo_recv, south_in_send, south_in_recv,
    out_send, out_recv, own_out, south_out_send, south_out_recv, own_in) = rest
    blocks, pitch, own, cols, lat = plan.blocks, plan.pitch, plan.own, plan.cols, plan.lat
    group, groups, slots = plan.group, plan.groups, plan.slots
    me = lax.axis_index("lon")
    band = lax.axis_index("lat")
    has_north = band < plan.bands - 1
    north = lax.rem(band + 1, plan.bands)

    has_south = band > 0
    barrier = pltpu.get_barrier_semaphore()
    for k in range(1, blocks):
        pl.semaphore_signal(
            barrier,
            inc=1,
            device_id={"lon": lax.rem(me + k, blocks), "lat": band},
            device_id_type=MESH,
        )
    for there, to in ((has_north, north), (has_south, lax.rem(band + plan.bands - 1, plan.bands))):

        @pl.when(there)
        def _():
            for k in range(blocks):
                pl.semaphore_signal(
                    barrier, inc=1, device_id={"lon": jnp.int32(k), "lat": to}, device_id_type=MESH
                )

    def lines(first, count):
        return pl.ds(pl.multiple_of(first * pitch, 8), count * pitch)

    def load(f):
        part = pl.ds(f * lat, lat)
        return pltpu.make_async_copy(x_ref.at[part], x_local.at[part], x_sem.at[f])

    start_all([load(f) for f in range(plan.fields)])
    table_copies = [
        pltpu.make_async_copy(source, to, table_sem.at[i])
        for i, (source, to) in enumerate(zip(inputs, tables))
    ]
    start_all(table_copies)
    packed[0 : HALO * pitch, :] = jnp.zeros((HALO * pitch, LANES), jnp.float32)

    def fill(part, none):
        for c in range(cols):
            width = LANES if c < cols - 1 else plan.rem
            v = x_local[pl.ds(pl.multiple_of(part * 8, 8), 8), c * LANES : c * LANES + width]
            if width < LANES:
                v = jnp.concatenate([v, jnp.zeros((8, LANES - width), jnp.float32)], axis=1)
            packed[pl.ds((part * 8 + HALO) * pitch + c, 8, stride=pitch), :] = v
        return none

    for f in range(plan.fields):
        load(f).wait()
        lax.fori_loop(f * (lat // 8), (f + 1) * (lat // 8), fill, 0)

    bands_met = jnp.where(has_north, 1, 0) + jnp.where(has_south, 1, 0)
    pl.semaphore_wait(barrier, blocks - 1 + blocks * bands_met)

    def peer(k):
        return lax.rem(me + k, blocks)

    def halo_in(k):
        return pltpu.make_async_remote_copy(
            src_ref=packed.at[lines(peer(k) * own, HALO)],
            dst_ref=arrived.at[lines(me * slots, HALO)],
            send_sem=halo_send.at[k],
            recv_sem=halo_recv.at[k],
            device_id={"lon": peer(k), "lat": band},
            device_id_type=MESH,
        )

    def group_in(k, g):
        return pltpu.make_async_remote_copy(
            src_ref=packed.at[lines(peer(k) * own + HALO + g * group, group)],
            dst_ref=arrived.at[lines(me * slots + HALO + g * group, group)],
            send_sem=in_send.at[k, g],
            recv_sem=in_recv.at[k, g],
            device_id={"lon": peer(k), "lat": band},
            device_id_type=MESH,
        )

    def south_in(i):
        f, d = plan.south_to[i]
        return pltpu.make_async_remote_copy(
            src_ref=packed.at[lines(HALO + f * lat + lat - HALO, HALO)],
            dst_ref=arrived.at[lines(me * slots + own + HALO, HALO)],
            send_sem=south_in_send.at[i],
            recv_sem=south_in_recv.at[me],
            device_id={"lon": jnp.int32(d), "lat": north},
            device_id_type=MESH,
        )

    local = pltpu.make_async_copy(
        packed.at[lines(me * own, own + HALO)], arrived.at[lines(me * slots, own + HALO)], own_in
    )
    local.start()
    start_all([halo_in(k) for k in range(1, blocks)])

    @pl.when(has_north)
    def _():
        start_all([south_in(i) for i in range(len(plan.south_to))])

    for g in range(groups):
        start_all([group_in(k, g) for k in range(1, blocks)])

    for copy in table_copies:
        copy.wait()

    def place(slot):
        flat = me * own + slot - HALO
        south = slot >= own + HALO
        row = jnp.where(south, slot - (own + 2 * HALO), lax.rem(flat + lat, lat))
        return south, jnp.maximum(band * lat + row, 0)

    def build(slot, none):
        build_weights(table, place(slot)[1], weights, slot)
        return none

    lax.fori_loop(0, slots, build, 0)
    for j in range(lat):
        for i, weight in enumerate(face_weights(plan, cy, SUBS - 1, band * lat + j)):
            coef[i, j : j + 1, :] = jnp.full((1, LANES), weight, jnp.float32)

    def steps(x, t, row, slot):
        return row_steps(
            plan,
            x,
            cx[t, 0, row],
            shift[t, 0, row],
            mask[row],
            lambda i: table[i, row],
            weights[slot],
        )

    def first_pass(slot):
        south, row = place(slot)
        x = [arrived[pl.ds(slot * pitch + c, blocks, stride=slots * pitch), :] for c in range(cols)]
        y = steps(x, 0, row, slot)
        outside = jnp.logical_and(south, band == 0)
        for c in range(cols):
            held[slot, :, c * LANES : (c + 1) * LANES] = jnp.where(outside, 0.0, y[c])

    def second_pass(m):
        j = lax.rem(me * own + m, lat)
        row = band * lat + j
        s0 = m + HALO
        s1 = jnp.where(j == 0, own + 3, s0 - 1)
        s2 = jnp.where(j == 0, own + 2, jnp.where(j == 1, own + 3, s0 - 2))
        a0, a1, a2 = face_weights(plan, cy, 0, row)
        x = []
        for c in range(cols):
            at = slice(c * LANES, (c + 1) * LANES)
            x.append(a0 * held[s0, :, at] + a1 * held[s1, :, at] + a2 * held[s2, :, at])
        y = steps(x, 1, row, s0)
        for c in range(cols):
            ready[pl.ds(m * pitch + c, blocks, stride=own * pitch), :] = y[c]

    def loop(count, each):
        width = 2 if count % 2 == 0 else 1

        def step(i, none):
            for part in range(width):
                each(i * width + part)
            return none

        lax.fori_loop(0, count // width, step, 0)

    def own_back(g):
        return pltpu.make_async_copy(
            ready.at[lines(me * own + g * group, group)],
            got.at[lines(me * own + g * group, group)],
            own_out.at[g],
        )

    def group_back(k, g):
        return pltpu.make_async_remote_copy(
            src_ref=ready.at[lines(peer(k) * own + g * group, group)],
            dst_ref=got.at[lines(me * own + g * group, group)],
            send_sem=out_send.at[k, g],
            recv_sem=out_recv.at[k, g],
            device_id={"lon": peer(k), "lat": band},
            device_id_type=MESH,
        )

    pieces = [(f, part) for f in range(plan.fields) for part in range(HALO // plan.unit)]

    def piece_row(i):
        f, part = pieces[i]
        return f * lat + lat - HALO + part * plan.unit

    def south_back(i, to):
        f, part = pieces[i]
        inside = piece_row(i) % own
        return pltpu.make_async_remote_copy(
            src_ref=ready.at[lines(to * own + inside, plan.unit)],
            dst_ref=got_south.at[lines(f * HALO + part * plan.unit, plan.unit)],
            send_sem=south_out_send.at[i, to],
            recv_sem=south_out_recv.at[i],
            device_id={"lon": jnp.int32(to), "lat": north},
            device_id_type=MESH,
        )

    def sends_south(i):
        return jnp.logical_and(has_north, me == piece_row(i) // own)

    local.wait()
    for k in range(1, blocks):
        halo_in(k).wait_recv()
    for d in sorted({d for _, d in plan.south_to}):

        @pl.when(jnp.logical_and(band > 0, me == d))
        def _():
            for source in range(blocks):
                pltpu.make_async_remote_copy(
                    src_ref=packed.at[lines(0, HALO)],
                    dst_ref=arrived.at[lines(source * slots + own + HALO, HALO)],
                    send_sem=south_in_send.at[0],
                    recv_sem=south_in_recv.at[source],
                    device_id={"lon": me, "lat": lax.rem(band + plan.bands - 1, plan.bands)},
                    device_id_type=MESH,
                ).wait_recv()

    loop(2 * HALO, lambda i: first_pass(jnp.where(i < HALO, i, i + own)))

    def one_group(g, none):
        for k in range(1, blocks):
            group_in(k, g).wait_recv()
        loop(group, lambda i: first_pass(HALO + g * group + i))
        loop(group, lambda i: second_pass(g * group + i))
        own_back(g).start()
        start_all([group_back(k, g) for k in range(1, blocks)])
        for i in range(len(pieces)):

            @pl.when(jnp.logical_and(sends_south(i), g == piece_row(i) % own // group))
            def _():
                start_all([south_back(i, to) for to in range(blocks)])

        return none

    lax.fori_loop(0, groups, one_group, 0)

    for k in range(1, blocks):
        halo_in(k).wait_send()
        for g in range(groups):
            group_in(k, g).wait_send()

    @pl.when(has_north)
    def _():
        for i in range(len(plan.south_to)):
            south_in(i).wait_send()

    for g in range(groups):
        own_back(g).wait()
        for k in range(1, blocks):
            group_back(k, g).wait()
    for i in range(len(pieces)):

        @pl.when(sends_south(i))
        def _():
            for to in range(blocks):
                south_back(i, to).wait_send()

    @pl.when(band > 0)
    def _():
        for i in range(len(pieces)):
            south_back(i, 0).wait_recv()

    @pl.when(band == 0)
    def _():
        got_south[...] = jnp.zeros_like(got_south)

    sub = lax.broadcasted_iota(jnp.int32, (8, LANES), 0)

    def one_field(f, none):
        for g in range(lat // 8):
            a0, a1, a2 = (coef[i, g * 8 : g * 8 + 8, :] for i in range(3))
            for c in range(cols):
                base = (f * lat + g * 8) * pitch + c
                x0 = got[pl.ds(base, 8, stride=pitch), :]
                if g:
                    x1 = got[pl.ds(base - pitch, 8, stride=pitch), :]
                    x2 = got[pl.ds(base - 2 * pitch, 8, stride=pitch), :]
                else:
                    south2 = got_south[pl.ds(f * HALO * pitch + c, 1), :]
                    south1 = got_south[pl.ds((f * HALO + 1) * pitch + c, 1), :]
                    x1 = jnp.where(sub == 0, south1, pltpu.roll(x0, 1, 0))
                    x2 = jnp.where(
                        sub == 0, south2, jnp.where(sub == 1, south1, pltpu.roll(x0, 2, 0))
                    )
                v = a0 * x0 + a1 * x1 + a2 * x2
                width = LANES if c < cols - 1 else plan.rem
                out_ref[f, 0, g * 8 : g * 8 + 8, c * LANES : c * LANES + width] = v[:, :width]
        return none

    lax.fori_loop(0, plan.fields, one_field, 0)


def body(plan, fields, frac_x, frac_y, shift_cells, polar_mask):
    blocks, pitch, own, lat = plan.blocks, plan.pitch, plan.own, plan.lat
    vmem = pl.BlockSpec(memory_space=pltpu.VMEM)
    anywhere = pl.BlockSpec(memory_space=pltpu.HBM)
    dma = pltpu.SemaphoreType.DMA
    n_pieces = plan.fields * (HALO // plan.unit)

    def lines(rows):
        return pltpu.VMEM((rows * pitch, LANES), jnp.float32)

    tables = (frac_x, frac_y, shift_cells, polar_mask, jnp.asarray(decay_table(plan)))
    return pl.pallas_call(
        functools.partial(kernel, plan),
        out_shape=jax.ShapeDtypeStruct(fields.shape, jnp.float32),
        in_specs=[anywhere] * 6,
        out_specs=vmem,
        scratch_shapes=[
            *[pltpu.SMEM(table.shape, table.dtype) for table in tables],
            pltpu.VMEM((plan.rows, plan.lon), jnp.float32),
            dma((plan.fields,)),
            dma((len(tables),)),
            lines(HALO + plan.rows),
            lines(blocks * plan.slots),
            pltpu.VMEM((plan.slots, blocks, plan.cols * LANES), jnp.float32),
            pltpu.VMEM((plan.slots, 2 * LANES, 2 * LANES), jnp.bfloat16),
            lines(blocks * own),
            lines(plan.rows),
            lines(plan.fields * HALO),
            pltpu.VMEM((3, lat, LANES), jnp.float32),
            dma((blocks, plan.groups)),
            dma((blocks, plan.groups)),
            dma((blocks,)),
            dma((blocks,)),
            dma((len(plan.south_to),)),
            dma((blocks,)),
            dma((blocks, plan.groups)),
            dma((blocks, plan.groups)),
            dma((plan.groups,)),
            dma((n_pieces, blocks)),
            dma((n_pieces,)),
            dma,
        ],
        compiler_params=pltpu.CompilerParams(
            collective_id=0, has_side_effects=True, vmem_limit_bytes=VMEM_LIMIT
        ),
        name="transport",
    )(
        *tables,
        fields.reshape(plan.rows, plan.lon),
    )


def solution(mesh):
    def whole(fields, frac_x, frac_y, shift_cells, polar_mask):
        return jax.shard_map(
            functools.partial(body, Plan(mesh, fields.shape)),
            mesh=mesh,
            in_specs=(P(None, None, "lat", "lon"), P(), P(), P(), P()),
            out_specs=P(None, None, "lat", "lon"),
            check_vma=False,
        )(fields, frac_x, frac_y, shift_cells, polar_mask)

    return whole
```
